32 devices in a mesh: mode: 8 (over y, x, core), space: 4 (over z).
Axes of the slice: x: 2, y: 2, z: 4, core: 2. Of those that a mesh axis runs over, the one named last changes fastest.
Arguments:
- left_modes: bfloat16 [512, 24, 512], P('mode', None, 'space'), may hold values from -6 to 6
- right_modes: bfloat16 [512, 24, 512], P('mode', None, 'space'), may hold values from -6 to 6
- momenta: int32 [8, 3], replicated, may hold values from -3 to 3
- spin_perm: int32 [8, 4], replicated, may hold values from 0 to 3, each once within a row
- spin_phase: int32 [8, 4], replicated, may hold values from 0 to 3
Outputs:
- fields: float32 [64, 512, 64], P('space', 'mode')
The draws below stay inside these ranges and needn't reach their ends.
Inputs may be any that keep to these rules, and one draw needn't show every extreme that they name: `spin_perm`: each row is a permutation of 0 to 3.
All inputs are finite; a program needn't handle non-finite values.
Results may differ from the reference program's by a relative error of at most 0.0028.
Values may be sent and summed in bfloat16 or wider, within the bound.
No kernel may reach another device: no remote copies, remote signals or barrier semaphores. Data moves between devices by JAX's collectives and lax.ppermute only.
A program may use at most 64 MiB of HBM per device.

```python
import math
import jax
import jax.numpy as jnp
from jax import lax

MODE_DEV = 64
MODES = 512
COMP = 24
STRUCTS = 8
CYCLE = 4
SITES = 512
LAT = 96
BOX = 16
PLANES = 64
N_MODE = 8


def with_ends(result, key, smallest, top_value):
    index_at = [jax.random.randint(jax.random.fold_in(key, axis), (), 0, length) for axis, length in enumerate(result.shape)]
    widest = result.shape.index(max(result.shape))
    beside = index_at[:widest] + [(index_at[widest] + 1) % result.shape[widest]] + index_at[widest + 1:]
    return result.at[tuple(index_at)].set(smallest).at[tuple(beside)].set(top_value)


def shard_levels(rng, dims, cuts, low, largest):
    def one(position, parts):
        steps = jax.random.uniform(jax.random.fold_in(jax.random.fold_in(rng, 6), position), (parts,), jnp.float32, low / len(cuts), largest / len(cuts))
        return jnp.repeat(jnp.exp(steps), dims[position] // parts).reshape((-1,) + (1,) * (len(dims) - position - 1))

    factor_of = one(*cuts[0])
    for cut in cuts[1:]:
        factor_of = factor_of * one(*cut)
    return factor_of


def scatter_about(own_key, shape, deviation, bound, pieces=(), kind=jnp.bfloat16):
    result = jax.random.normal(own_key, shape, jnp.float32) * deviation
    if len(pieces) > 0:
        result = shard_levels(own_key, shape, pieces, -0.22, 0.18) * result
    return jnp.clip(result, min=-bound, max=bound).astype(kind)


def setup_inputs(seed: int = 0) -> dict:
    seeds = jax.random.split(jax.random.key(seed), 6)
    return {
        "left_modes": scatter_about(seeds[0], (MODES, COMP, SITES), 1.0, 6.0, ((0, 8), (2, 4))),
        "right_modes": scatter_about(seeds[1], (MODES, COMP, SITES), 1.0, 6.0, ((0, 8), (2, 4))),
        "momenta": with_ends(jax.random.randint(seeds[2], (STRUCTS, 3), -3, 4), jax.random.fold_in(seeds[2], 1), -3, 3).astype(jnp.int32),
        "spin_perm": jax.vmap(lambda own: jax.random.permutation(own, 4))(jax.random.split(seeds[3], STRUCTS)).reshape((STRUCTS, 4)).astype(jnp.int32),
        "spin_phase": with_ends(jax.random.randint(seeds[4], (STRUCTS, 4), 0, 4), jax.random.fold_in(seeds[4], 1), 0, 3).astype(jnp.int32),
    }


def turned_rows(mode_rows, momenta, spin_perm, spin_phase, coords, struct_id):
    mode_count = mode_rows.shape[0]
    site_count = mode_rows.shape[2]
    real_part = mode_rows[:, :12, :].astype(jnp.float32).reshape(mode_count, 4, 3, site_count)
    imag_part = mode_rows[:, 12:, :].astype(jnp.float32).reshape(mode_count, 4, 3, site_count)
    momentum_dot = lax.optimization_barrier(jnp.sum(momenta[struct_id][:, None] * coords, axis=0))
    quarter = jnp.mod(LAT // 4 * spin_phase[struct_id][:, None] - momentum_dot[None, :], LAT)
    phase_angle = quarter.astype(jnp.float32) * (2.0 * math.pi / LAT)
    cosine = jnp.cos(phase_angle)[None, :, None, :]
    sine_val = jnp.sin(phase_angle)[None, :, None, :]
    turn_re = real_part * cosine + imag_part * sine_val
    turn_im = imag_part * cosine - real_part * sine_val
    chooser = (spin_perm[struct_id][:, None] == jnp.arange(4, dtype=jnp.int32)[None, :]).astype(jnp.float32)
    moved_re = jnp.einsum('ab,iacs->ibcs', chooser, turn_re, precision=lax.Precision.HIGHEST)
    moved_im = jnp.einsum('ab,iacs->ibcs', chooser, turn_im, precision=lax.Precision.HIGHEST)
    re_rows = jnp.concatenate([moved_re, moved_im], axis=1).reshape(mode_count, 24, site_count)
    im_rows = jnp.concatenate([-moved_im, moved_re], axis=1).reshape(mode_count, 24, site_count)
    stacked = jnp.stack([re_rows, im_rows]).astype(jnp.bfloat16)
    return stacked.reshape(2 * mode_count, 24 * site_count)

def reference(left_modes, right_modes, momenta, spin_perm, spin_phase):
    site_index = lax.iota(jnp.int32, SITES)
    coords = jnp.stack([site_index % BOX, site_index // BOX % BOX, site_index // (BOX * BOX)])
    left_blocks = left_modes.reshape(N_MODE, MODE_DEV, 24, SITES)
    right_blocks = right_modes.reshape(N_MODE, MODE_DEV, 24, SITES)

    def block_field(block_id):
        left_here = lax.dynamic_index_in_dim(left_blocks, block_id, 0, keepdims=False)
        rights = jnp.stack([lax.dynamic_index_in_dim(right_blocks, jnp.mod(block_id - shift_step, N_MODE).astype(jnp.int32), 0, keepdims=False) for shift_step in range(CYCLE)]).reshape(CYCLE * MODE_DEV, 24 * SITES)
        planes = []
        for struct_id in range(STRUCTS):
            rows_here = turned_rows(left_here, momenta, spin_perm, spin_phase, coords, struct_id)
            product = jnp.dot(rows_here, rights.T, preferred_element_type=jnp.float32)
            planes.append(product.reshape(2, MODE_DEV, CYCLE, MODE_DEV).transpose(2, 0, 1, 3))
        return jnp.stack(planes)
    fields = lax.map(block_field, jnp.arange(N_MODE, dtype=jnp.int32))
    fields = fields.transpose(1, 2, 3, 0, 4, 5).reshape(PLANES, MODES, MODE_DEV)
    return fields * (1.0 / math.sqrt(24 * SITES))
```

```python
import functools
import math

import jax
import jax.numpy as jnp
from jax import lax
from jax.experimental import pallas as pl
from jax.experimental.pallas import tpu as pltpu
from jax.sharding import PartitionSpec as P


STRUCTS = 8
CYCLE = 4
LAT = 96
BOX = 16
LANES = 128
F32 = jnp.float32
BF16 = jnp.bfloat16
VMEM = pl.BlockSpec(memory_space=pltpu.VMEM)
SMEM = pl.BlockSpec(memory_space=pltpu.SMEM)
PARAMS = pltpu.CompilerParams(vmem_limit_bytes=16 << 20)


def routed(block, axis, source):
    size = lax.axis_size(axis)
    return lax.ppermute(block, axis, [(source(i) % size, i) for i in range(size)])


def build_rows(left, momenta, perm, phase, angle, cosine, sine, rows):
    modes = left.shape[0]
    structs = momenta.shape[1]
    sites = left.shape[1] // 24
    half = 12 * sites
    site = lax.axis_index("space") * sites + lax.broadcasted_iota(jnp.int32, (1, sites), 1)
    x = (site % BOX).astype(F32)
    y = (site // BOX % BOX).astype(F32)
    z = (site // (BOX * BOX)).astype(F32)
    for g in range(structs):
        dot = momenta[0, g].astype(F32) * x + momenta[1, g].astype(F32) * y + momenta[2, g].astype(F32) * z
        for a in range(4):
            angle[g * 4 + a : g * 4 + a + 1, :] = (LAT // 4 * phase[a, g]).astype(F32) - dot
    steps = angle[...]
    steps = steps - LAT * jnp.floor(steps * (1.0 / LAT))
    psi = steps * (2.0 * math.pi / LAT)
    cosine[...] = jnp.cos(psi)
    sine[...] = jnp.sin(psi)
    for a in range(4):
        for k in range(3):
            at = (a * 3 + k) * sites
            re = left[:, at : at + sites].astype(F32)
            im = left[:, half + at : half + at + sites].astype(F32)
            for g in range(structs):
                co = cosine[g * 4 + a : g * 4 + a + 1, :]
                si = sine[g * 4 + a : g * 4 + a + 1, :]
                to = pl.multiple_of((perm[a, g] * 3 + k) * sites, LANES)
                rows[g * modes : (g + 1) * modes, pl.ds(to, sites)] = (re * co + im * si).astype(BF16)
                to = pl.multiple_of(half + (perm[a, g] * 3 + k) * sites, LANES)
                rows[g * modes : (g + 1) * modes, pl.ds(to, sites)] = (im * co - re * si).astype(BF16)


def multiply(rows, right, both, total, sends, kept):
    modes, depth = right.shape
    half = depth // 2
    both[0:modes, :] = right[...]
    both[modes:, 0:half] = right[:, half:]
    both[modes:, half:] = -right[:, 0:half]
    total[...] = lax.dot_general(
        rows[...], both[...], (((1,), (1,)), ((), ())), preferred_element_type=F32
    ).reshape(total.shape)
    me = lax.axis_index("space")
    own = kept.shape[0]
    kept[...] = total[pl.ds(me * own, own)]
    for distance, send in enumerate(sends, 1):
        send[...] = total[pl.ds((me ^ distance) * own, own)].astype(BF16)


def first_kernel(n_send, left, right, momenta, perm, phase, rows, kept, *rest):
    sends, (angle, cosine, sine, both, total) = rest[:n_send], rest[n_send:]
    build_rows(left, momenta, perm, phase, angle, cosine, sine, rows)
    multiply(rows, right, both, total, sends, kept)


def next_kernel(n_send, rows, right, kept, *rest):
    sends, (both, total) = rest[:n_send], rest[n_send:]
    multiply(rows, right, both, total, sends, kept)


def join_kernel(groups, factor, *refs):
    out = refs[-1]
    each = (len(refs) - 1) // groups
    odd = lax.axis_index("mode") % 2
    places = (0, 1 + 2 * odd, 2, 3 - 2 * odd)
    modes = out.shape[1]
    for place, start in zip(places, range(0, groups * each, each)):
        for g in range(refs[start].shape[0]):
            value = refs[start][g]
            for part in refs[start + 1 : start + each]:
                value = value + part[g].astype(F32)
            value = value * factor
            for p in range(2):
                out[(g * CYCLE + place) * 2 + p] = value[:, p * modes : (p + 1) * modes]


def local(left_modes, right_modes, momenta, spin_perm, spin_phase):
    modes, comps, sites = left_modes.shape
    spaces = lax.axis_size("space")
    depth = comps * sites
    own = STRUCTS // spaces
    n_send = spaces - 1
    shape = jax.ShapeDtypeStruct
    outs = [shape((own, modes, 2 * modes), F32)] + [shape((own, modes, 2 * modes), BF16)] * n_send
    work = [pltpu.VMEM((2 * modes, depth), BF16), pltpu.VMEM((STRUCTS, modes, 2 * modes), F32)]

    ahead = routed(right_modes, "mode", lambda i: i - 1 if i % 2 == 0 else i - 3)
    far = routed(right_modes, "mode", lambda i: i - 3 if i % 2 == 0 else i - 1)
    swapped = routed(ahead, "mode", lambda i: i ^ 1)

    def exchange(group):
        kept, *sends = group
        return [kept] + [routed(s, "space", lambda i, d=d: i ^ d) for d, s in enumerate(sends, 1)]

    rows, *group = pl.pallas_call(
        functools.partial(first_kernel, n_send),
        out_shape=[shape((STRUCTS * modes, depth), BF16)] + outs,
        in_specs=[VMEM, VMEM, SMEM, SMEM, SMEM],
        out_specs=[VMEM] * (2 + n_send),
        scratch_shapes=[pltpu.VMEM((4 * STRUCTS, sites), F32)] * 3 + work,
        compiler_params=PARAMS,
        name="first",
    )(left_modes.reshape(modes, depth), right_modes.reshape(modes, depth), momenta.T, spin_perm.T, spin_phase.T)
    received = exchange(group)
    for block in (ahead, swapped, far):
        group = pl.pallas_call(
            functools.partial(next_kernel, n_send),
            out_shape=outs,
            in_specs=[VMEM, VMEM],
            out_specs=[VMEM] * (1 + n_send),
            scratch_shapes=work,
            compiler_params=PARAMS,
            name="next",
        )(rows, block.reshape(modes, depth))
        received += exchange(group)
    return pl.pallas_call(
        functools.partial(join_kernel, CYCLE, 1.0 / math.sqrt(depth * spaces)),
        out_shape=shape((own * CYCLE * 2, modes, modes), F32),
        in_specs=[VMEM] * len(received),
        out_specs=VMEM,
        compiler_params=PARAMS,
        name="join",
    )(*received)


def turned_rows(mode_rows, momenta, spin_perm, spin_phase, coords, struct_id):
    mode_count = mode_rows.shape[0]
    site_count = mode_rows.shape[2]
    real_part = mode_rows[:, :12, :].astype(F32).reshape(mode_count, 4, 3, site_count)
    imag_part = mode_rows[:, 12:, :].astype(F32).reshape(mode_count, 4, 3, site_count)
    momentum_dot = jnp.sum(momenta[struct_id][:, None] * coords, axis=0)
    quarter = jnp.mod(LAT // 4 * spin_phase[struct_id][:, None] - momentum_dot[None, :], LAT)
    phase_angle = quarter.astype(F32) * (2.0 * math.pi / LAT)
    cosine = jnp.cos(phase_angle)[None, :, None, :]
    sine_val = jnp.sin(phase_angle)[None, :, None, :]
    turn_re = real_part * cosine + imag_part * sine_val
    turn_im = imag_part * cosine - real_part * sine_val
    chooser = (spin_perm[struct_id][:, None] == jnp.arange(4, dtype=jnp.int32)[None, :]).astype(F32)
    moved_re = chooser[0][None, :, None, None] * turn_re[:, 0:1]
    moved_im = chooser[0][None, :, None, None] * turn_im[:, 0:1]
    for a in range(1, 4):
        moved_re = moved_re + chooser[a][None, :, None, None] * turn_re[:, a : a + 1]
        moved_im = moved_im + chooser[a][None, :, None, None] * turn_im[:, a : a + 1]
    re_rows = jnp.concatenate([moved_re, moved_im], axis=1).reshape(mode_count, 24, site_count)
    im_rows = jnp.concatenate([-moved_im, moved_re], axis=1).reshape(mode_count, 24, site_count)
    return jnp.stack([re_rows, im_rows]).astype(BF16).reshape(2 * mode_count, 24 * site_count)


def plain_local(left_modes, right_modes, momenta, spin_perm, spin_phase):
    mode_count, comp_count, site_count = left_modes.shape
    space_count = lax.axis_size("space")
    site_index = lax.axis_index("space") * site_count + lax.iota(jnp.int32, site_count)
    coords = jnp.stack([site_index % BOX, site_index // BOX % BOX, site_index // (BOX * BOX)])
    blocks = [right_modes]
    for _ in range(1, CYCLE):
        blocks.append(routed(blocks[-1], "mode", lambda i: i - 1))
    rights = jnp.stack(blocks).reshape(CYCLE * mode_count, comp_count * site_count)
    all_rows = jnp.concatenate(
        [turned_rows(left_modes, momenta, spin_perm, spin_phase, coords, g) for g in range(STRUCTS)], axis=0
    )
    product = lax.dot_general(all_rows, rights, (((1,), (1,)), ((), ())), preferred_element_type=F32)
    partial_value = product.reshape(STRUCTS, 2, mode_count, CYCLE, mode_count).transpose(0, 3, 1, 2, 4)
    partial_value = partial_value.reshape(STRUCTS * CYCLE * 2, mode_count, mode_count)
    owned = lax.psum_scatter(partial_value, "space", scatter_dimension=0, tiled=True)
    return owned * (1.0 / math.sqrt(24 * site_count * space_count))


def solution(mesh):
    spaces, n_mode = mesh.shape["space"], mesh.shape["mode"]
    fits = spaces & (spaces - 1) == 0 and STRUCTS % spaces == 0 and n_mode % 2 == 0 and n_mode >= CYCLE

    def either(left_modes, *rest):
        body = local if fits and left_modes.shape[2] % LANES == 0 else plain_local
        return body(left_modes, *rest)

    placed = (P("mode", None, "space"), P("mode", None, "space"), P(), P(), P())
    return jax.shard_map(
        either, mesh=mesh, in_specs=placed, out_specs=P("space", "mode", None), check_vma=False
    )
```

```python
import functools
import math

import jax
import jax.numpy as jnp
from jax import lax
from jax.experimental import pallas as pl
from jax.experimental.pallas import tpu as pltpu
from jax.sharding import PartitionSpec as P


STRUCTS = 8
CYCLE = 4
LAT = 96
BOX = 16
LANES = 128
F32 = jnp.float32
BF16 = jnp.bfloat16
VMEM = pl.BlockSpec(memory_space=pltpu.VMEM)
SMEM = pl.BlockSpec(memory_space=pltpu.SMEM)
PARAMS = pltpu.CompilerParams(vmem_limit_bytes=16 << 20)


def routed(block, axis, source):
    size = lax.axis_size(axis)
    return lax.ppermute(block, axis, [(source(i) % size, i) for i in range(size)])


def build_rows(left, momenta, perm, phase, angle, cosine, sine, rows):
    modes = left.shape[0]
    structs = momenta.shape[1]
    sites = left.shape[1] // 24
    half = 12 * sites
    site = lax.axis_index("space") * sites + lax.broadcasted_iota(jnp.int32, (1, sites), 1)
    x = (site % BOX).astype(F32)
    y = (site // BOX % BOX).astype(F32)
    z = (site // (BOX * BOX)).astype(F32)
    for g in range(structs):
        dot = momenta[0, g].astype(F32) * x + momenta[1, g].astype(F32) * y + momenta[2, g].astype(F32) * z
        for a in range(4):
            angle[g * 4 + a : g * 4 + a + 1, :] = (LAT // 4 * phase[a, g]).astype(F32) - dot
    steps = angle[...]
    steps = steps - LAT * jnp.floor(steps * (1.0 / LAT))
    psi = steps * (2.0 * math.pi / LAT)
    cosine[...] = jnp.cos(psi)
    sine[...] = jnp.sin(psi)
    for a in range(4):
        for k in range(3):
            at = (a * 3 + k) * sites
            re = left[:, at : at + sites].astype(F32)
            im = left[:, half + at : half + at + sites].astype(F32)
            for g in range(structs):
                co = cosine[g * 4 + a : g * 4 + a + 1, :]
                si = sine[g * 4 + a : g * 4 + a + 1, :]
                to = pl.multiple_of((perm[a, g] * 3 + k) * sites, LANES)
                rows[g * modes : (g + 1) * modes, pl.ds(to, sites)] = (re * co + im * si).astype(BF16)
                to = pl.multiple_of(half + (perm[a, g] * 3 + k) * sites, LANES)
                rows[g * modes : (g + 1) * modes, pl.ds(to, sites)] = (im * co - re * si).astype(BF16)


def multiply(rows, right, both, total, sends, kept, slot=0):
    modes, depth = right.shape
    half = depth // 2
    both[0:modes, :] = right[...]
    both[modes:, 0:half] = right[:, half:]
    both[modes:, half:] = -right[:, 0:half]
    total[...] = lax.dot_general(
        rows[...], both[...], (((1,), (1,)), ((), ())), preferred_element_type=F32
    ).reshape(total.shape)
    me = lax.axis_index("space")
    own = kept.shape[1]
    kept[slot] = total[pl.ds(me * own, own)]
    for distance, send in enumerate(sends, 1):
        send[slot] = total[pl.ds((me ^ distance) * own, own)].astype(BF16)


def first_kernel(n_send, left, right, momenta, perm, phase, rows, kept, *rest):
    sends, (angle, cosine, sine, both, total) = rest[:n_send], rest[n_send:]
    build_rows(left, momenta, perm, phase, angle, cosine, sine, rows)
    multiply(rows, right, both, total, sends, kept)


def next_kernel(n_send, rows, right, kept, *rest):
    sends, (both, total) = rest[:n_send], rest[n_send:]
    multiply(rows, right, both, total, sends, kept)


def add_kernel(n_send, rows, right, *rest):
    before, after, (both, total) = rest[: 1 + n_send], rest[1 + n_send : 2 + 2 * n_send], rest[2 + 2 * n_send :]
    for old, new in zip(before, after):
        new[0:1] = old[...]
    multiply(rows, right, both, total, after[1:], after[0], 1)


def join_kernel(spaces, factor, *refs):
    out = refs[-1]
    odd = lax.axis_index("mode") % 2
    places = iter((0, 1 + 2 * odd, 2, 3 - 2 * odd))
    modes = out.shape[1]
    for start in range(0, len(refs) - 1, spaces):
        for slot in range(refs[start].shape[0]):
            place = next(places)
            for g in range(refs[start].shape[1]):
                value = refs[start][slot, g]
                for part in refs[start + 1 : start + spaces]:
                    value = value + part[slot, g].astype(F32)
                value = value * factor
                for p in range(2):
                    out[(g * CYCLE + place) * 2 + p] = value[:, p * modes : (p + 1) * modes]


def local(left_modes, right_modes, momenta, spin_perm, spin_phase):
    modes, comps, sites = left_modes.shape
    spaces = lax.axis_size("space")
    depth = comps * sites
    own = STRUCTS // spaces
    n_send = spaces - 1
    shape = jax.ShapeDtypeStruct

    def outs(slots):
        size = (slots, own, modes, 2 * modes)
        return [shape(size, F32)] + [shape(size, BF16)] * n_send

    work = [pltpu.VMEM((2 * modes, depth), BF16), pltpu.VMEM((STRUCTS, modes, 2 * modes), F32)]

    ahead = routed(right_modes, "mode", lambda i: i - 1 if i % 2 == 0 else i - 3)
    far = routed(right_modes, "mode", lambda i: i - 3 if i % 2 == 0 else i - 1)
    swapped = routed(ahead, "mode", lambda i: i ^ 1)

    def exchange(group):
        kept, *sends = group
        return [kept] + [routed(s, "space", lambda i, d=d: i ^ d) for d, s in enumerate(sends, 1)]

    rows, *group = pl.pallas_call(
        functools.partial(first_kernel, n_send),
        out_shape=[shape((STRUCTS * modes, depth), BF16)] + outs(1),
        in_specs=[VMEM, VMEM, SMEM, SMEM, SMEM],
        out_specs=[VMEM] * (2 + n_send),
        scratch_shapes=[pltpu.VMEM((4 * STRUCTS, sites), F32)] * 3 + work,
        compiler_params=PARAMS,
        name="first",
    )(left_modes.reshape(modes, depth), right_modes.reshape(modes, depth), momenta.T, spin_perm.T, spin_phase.T)
    received = exchange(group)

    def product(kernel, slots, block, *before):
        return pl.pallas_call(
            functools.partial(kernel, n_send),
            out_shape=outs(slots),
            in_specs=[VMEM] * (2 + len(before)),
            out_specs=[VMEM] * (1 + n_send),
            scratch_shapes=work,
            compiler_params=PARAMS,
        )(rows, block.reshape(modes, depth), *before)

    group = product(next_kernel, 1, ahead)
    received += exchange(product(add_kernel, 2, swapped, *group))
    received += exchange(product(next_kernel, 1, far))
    return pl.pallas_call(
        functools.partial(join_kernel, spaces, 1.0 / math.sqrt(depth * spaces)),
        out_shape=shape((own * CYCLE * 2, modes, modes), F32),
        in_specs=[VMEM] * len(received),
        out_specs=VMEM,
        compiler_params=PARAMS,
        name="join",
    )(*received)


def turned_rows(mode_rows, momenta, spin_perm, spin_phase, coords, struct_id):
    mode_count = mode_rows.shape[0]
    site_count = mode_rows.shape[2]
    real_part = mode_rows[:, :12, :].astype(F32).reshape(mode_count, 4, 3, site_count)
    imag_part = mode_rows[:, 12:, :].astype(F32).reshape(mode_count, 4, 3, site_count)
    momentum_dot = jnp.sum(momenta[struct_id][:, None] * coords, axis=0)
    quarter = jnp.mod(LAT // 4 * spin_phase[struct_id][:, None] - momentum_dot[None, :], LAT)
    phase_angle = quarter.astype(F32) * (2.0 * math.pi / LAT)
    cosine = jnp.cos(phase_angle)[None, :, None, :]
    sine_val = jnp.sin(phase_angle)[None, :, None, :]
    turn_re = real_part * cosine + imag_part * sine_val
    turn_im = imag_part * cosine - real_part * sine_val
    chooser = (spin_perm[struct_id][:, None] == jnp.arange(4, dtype=jnp.int32)[None, :]).astype(F32)
    moved_re = chooser[0][None, :, None, None] * turn_re[:, 0:1]
    moved_im = chooser[0][None, :, None, None] * turn_im[:, 0:1]
    for a in range(1, 4):
        moved_re = moved_re + chooser[a][None, :, None, None] * turn_re[:, a : a + 1]
        moved_im = moved_im + chooser[a][None, :, None, None] * turn_im[:, a : a + 1]
    re_rows = jnp.concatenate([moved_re, moved_im], axis=1).reshape(mode_count, 24, site_count)
    im_rows = jnp.concatenate([-moved_im, moved_re], axis=1).reshape(mode_count, 24, site_count)
    return jnp.stack([re_rows, im_rows]).astype(BF16).reshape(2 * mode_count, 24 * site_count)


def plain_local(left_modes, right_modes, momenta, spin_perm, spin_phase):
    mode_count, comp_count, site_count = left_modes.shape
    space_count = lax.axis_size("space")
    site_index = lax.axis_index("space") * site_count + lax.iota(jnp.int32, site_count)
    coords = jnp.stack([site_index % BOX, site_index // BOX % BOX, site_index // (BOX * BOX)])
    blocks = [right_modes]
    for _ in range(1, CYCLE):
        blocks.append(routed(blocks[-1], "mode", lambda i: i - 1))
    rights = jnp.stack(blocks).reshape(CYCLE * mode_count, comp_count * site_count)
    all_rows = jnp.concatenate(
        [turned_rows(left_modes, momenta, spin_perm, spin_phase, coords, g) for g in range(STRUCTS)], axis=0
    )
    product = lax.dot_general(all_rows, rights, (((1,), (1,)), ((), ())), preferred_element_type=F32)
    partial_value = product.reshape(STRUCTS, 2, mode_count, CYCLE, mode_count).transpose(0, 3, 1, 2, 4)
    partial_value = partial_value.reshape(STRUCTS * CYCLE * 2, mode_count, mode_count)
    owned = lax.psum_scatter(partial_value, "space", scatter_dimension=0, tiled=True)
    return owned * (1.0 / math.sqrt(24 * site_count * space_count))


def solution(mesh):
    spaces, n_mode = mesh.shape["space"], mesh.shape["mode"]
    fits = spaces & (spaces - 1) == 0 and STRUCTS % spaces == 0 and n_mode % 2 == 0 and n_mode >= CYCLE

    def either(left_modes, *rest):
        body = local if fits and left_modes.shape[2] % LANES == 0 else plain_local
        return body(left_modes, *rest)

    placed = (P("mode", None, "space"), P("mode", None, "space"), P(), P(), P())
    return jax.shard_map(
        either, mesh=mesh, in_specs=placed, out_specs=P("space", "mode", None), check_vma=False
    )
```

```python
import functools
import math

import jax
import jax.numpy as jnp
from jax import lax
from jax.experimental import pallas as pl
from jax.experimental.pallas import tpu as pltpu
from jax.sharding import PartitionSpec as P


STRUCTS = 8
CYCLE = 4
LAT = 96
BOX = 16
LANES = 128
F32 = jnp.float32
BF16 = jnp.bfloat16
VMEM = pl.BlockSpec(memory_space=pltpu.VMEM)
HBM = pl.BlockSpec(memory_space=pltpu.HBM)
PARAMS = pltpu.CompilerParams(vmem_limit_bytes=16 << 20)


def routed(block, axis, source):
    size = lax.axis_size(axis)
    return lax.ppermute(block, axis, [(source(i) % size, i) for i in range(size)])


def turn_tables(momenta, phase, angle, cosine, sine):
    sites = angle.shape[1]
    site = lax.axis_index("space") * sites + lax.broadcasted_iota(jnp.int32, (1, sites), 1)
    x = (site % BOX).astype(F32)
    y = (site // BOX % BOX).astype(F32)
    z = (site // (BOX * BOX)).astype(F32)
    for g in range(momenta.shape[1]):
        dot = momenta[0, g].astype(F32) * x + momenta[1, g].astype(F32) * y + momenta[2, g].astype(F32) * z
        for a in range(4):
            angle[g * 4 + a : g * 4 + a + 1, :] = (LAT // 4 * phase[a, g]).astype(F32) - dot
    steps = angle[...]
    steps = steps - LAT * jnp.floor(steps * (1.0 / LAT))
    psi = steps * (2.0 * math.pi / LAT)
    cosine[...] = jnp.cos(psi)
    sine[...] = jnp.sin(psi)


def turn_rows(left, perm, cosine, sine, rows):
    modes = left.shape[0]
    sites = cosine.shape[1]
    half = 12 * sites
    for a in range(4):
        for k in range(3):
            at = (a * 3 + k) * sites
            re = left[:, at : at + sites].astype(F32)
            im = left[:, half + at : half + at + sites].astype(F32)
            for g in range(perm.shape[1]):
                co = cosine[g * 4 + a : g * 4 + a + 1, :]
                si = sine[g * 4 + a : g * 4 + a + 1, :]
                to = pl.multiple_of((perm[a, g] * 3 + k) * sites, LANES)
                rows[g * modes : (g + 1) * modes, pl.ds(to, sites)] = (re * co + im * si).astype(BF16)
                to = pl.multiple_of(half + (perm[a, g] * 3 + k) * sites, LANES)
                rows[g * modes : (g + 1) * modes, pl.ds(to, sites)] = (im * co - re * si).astype(BF16)


def flatten(block, flat):
    for at in range(0, block.shape[0], 16):
        flat[at : at + 16, :] = block[at : at + 16].reshape(16, flat.shape[1])


def multiply(all_rows, right, both, total, kept, sends):
    modes, depth = right.shape
    half = depth // 2
    both[0:modes, :] = right[...]
    both[modes:, 0:half] = right[:, half:]
    both[modes:, half:] = -right[:, 0:half]
    me = lax.axis_index("space")
    own = kept.shape[1]
    for slot, rows in enumerate(all_rows):
        total[...] = lax.dot_general(
            rows[...], both[...], (((1,), (1,)), ((), ())), preferred_element_type=F32
        ).reshape(total.shape)
        kept[slot] = total[pl.ds(me * own, own)]
        for distance, send in enumerate(sends, 1):
            send[slot] = total[pl.ds((me ^ distance) * own, own)].astype(BF16)


def first_kernel(n_send, left, right, momenta, perm, phase, rows, cosine, sine, kept, *rest):
    sends, (both, total, angle, lefts, rights, flat, *tables, done) = rest[:n_send], rest[n_send:]
    pairs = list(zip((momenta, perm, phase, left, right), (*tables, lefts, rights)))
    copies = [pltpu.make_async_copy(source, target, done.at[i]) for i, (source, target) in enumerate(pairs)]
    for copy in copies:
        copy.start()
    for copy in copies[:-1]:
        copy.wait()
    turn_tables(tables[0], tables[2], angle, cosine, sine)
    flatten(lefts, flat)
    turn_rows(flat, tables[1], cosine, sine, rows)
    copies[-1].wait()
    flatten(rights, flat)
    multiply((rows,), flat, both, total, kept, sends)


def other_kernel(left, perm, cosine, sine, rows, flat, table, done):
    copy = pltpu.make_async_copy(perm, table, done)
    copy.start()
    flatten(left, flat)
    copy.wait()
    turn_rows(flat, table, cosine, sine, rows)


def product_kernel(n_rows, *refs):
    all_rows, (right, kept, *sends, both, total) = refs[:n_rows], refs[n_rows:]
    multiply(all_rows, right, both, total, kept, sends)


def summed(parts, slot, g, factor):
    value = parts[0][slot, g]
    for part in parts[1:]:
        value = value + part[slot, g].astype(F32)
    return value * factor


def join_kernel(spaces, factor, *refs):
    early, middle, (out, other) = refs[:spaces], refs[spaces : 2 * spaces], refs[2 * spaces :]
    odd = lax.axis_index("mode") % 2
    modes = out.shape[1]
    for g in range(other.shape[0]):
        other[g] = summed(middle, 1, g, factor)
        for parts, place in ((early, 0), (middle, 1 + 2 * odd)):
            value = summed(parts, 0, g, factor)
            for p in range(2):
                out[(g * CYCLE + place) * 2 + p] = value[:, p * modes : (p + 1) * modes]


def last_kernel(factor, swapped, *refs):
    late, (_, out, planes, done) = refs[:-4], refs[-4:]
    odd = lax.axis_index("mode") % 2
    modes = out.shape[1]
    copies = []
    for g in range(swapped.shape[0]):
        for n, place in enumerate((2, 3 - 2 * odd)):
            value = swapped[g] if n == 0 else summed(late, 0, g, factor)
            for p in range(2):
                planes[g, n, p] = value[:, p * modes : (p + 1) * modes]
            to = out.at[pl.ds((g * CYCLE + place) * 2, 2)]
            copies.append(pltpu.make_async_copy(planes.at[g, n], to, done.at[2 * g + n]))
            copies[-1].start()
    for copy in copies:
        copy.wait()


def local(left_modes, right_modes, momenta, spin_perm, spin_phase):
    modes, comps, sites = left_modes.shape
    spaces = lax.axis_size("space")
    depth = comps * sites
    own = STRUCTS // spaces
    n_send = spaces - 1
    shape = jax.ShapeDtypeStruct

    def outs(slots):
        size = (slots, own, modes, 2 * modes)
        return [shape(size, F32)] + [shape(size, BF16)] * n_send

    work = [pltpu.VMEM((2 * modes, depth), BF16), pltpu.VMEM((STRUCTS, modes, 2 * modes), F32)]

    ahead = routed(right_modes, "mode", lambda i: i - 1 if i % 2 == 0 else i - 3)
    other_left = routed(left_modes, "mode", lambda i: i ^ 1)
    far = routed(right_modes, "mode", lambda i: i - 3 if i % 2 == 0 else i - 1)
    in_hbm = [pltpu.with_memory_space_constraint(t, pltpu.HBM) for t in (left_modes, right_modes)]
    tables = [pltpu.with_memory_space_constraint(t.T, pltpu.HBM) for t in (momenta, spin_perm, spin_phase)]
    table_shapes = [pltpu.SMEM(t.shape, jnp.int32) for t in tables]
    flat = pltpu.VMEM((modes, depth), BF16)
    rows_shape = shape((STRUCTS * modes, depth), BF16)
    turn_shape = shape((4 * STRUCTS, sites), F32)

    def exchange(group):
        kept, *sends = group
        return [kept] + [routed(s, "space", lambda i, d=d: i ^ d) for d, s in enumerate(sends, 1)]

    def product(all_rows, block):
        return pl.pallas_call(
            functools.partial(product_kernel, len(all_rows)),
            out_shape=outs(len(all_rows)),
            in_specs=[VMEM] * (len(all_rows) + 1),
            out_specs=[VMEM] * spaces,
            scratch_shapes=work,
            compiler_params=PARAMS,
        )(*all_rows, block.reshape(modes, depth))

    rows, cosine, sine, *group = pl.pallas_call(
        functools.partial(first_kernel, n_send),
        out_shape=[rows_shape, turn_shape, turn_shape] + outs(1),
        in_specs=[HBM] * 5,
        out_specs=[VMEM] * (3 + spaces),
        scratch_shapes=work
        + [pltpu.VMEM(turn_shape.shape, F32)]
        + [pltpu.VMEM(left_modes.shape, BF16)] * 2
        + [flat]
        + table_shapes
        + [pltpu.SemaphoreType.DMA((5,))],
        compiler_params=PARAMS,
        name="first",
    )(*in_hbm, *tables)
    early = exchange(group)
    other_rows = pl.pallas_call(
        other_kernel,
        out_shape=rows_shape,
        in_specs=[VMEM, HBM, VMEM, VMEM],
        out_specs=VMEM,
        scratch_shapes=[flat, table_shapes[1], pltpu.SemaphoreType.DMA],
        compiler_params=PARAMS,
        name="other",
    )(other_left, tables[1], cosine, sine)
    middle = exchange(product((rows, other_rows), ahead))
    late = exchange(product((rows,), far))
    factor = 1.0 / math.sqrt(depth * spaces)
    result = shape((own * CYCLE * 2, modes, modes), F32)
    out, other = pl.pallas_call(
        functools.partial(join_kernel, spaces, factor),
        out_shape=[result, shape((own, modes, 2 * modes), F32)],
        in_specs=[VMEM] * (2 * spaces),
        out_specs=[VMEM] * 2,
        compiler_params=PARAMS,
        name="join",
    )(*early, *middle)
    swapped = routed(other, "mode", lambda i: i ^ 1)
    return pl.pallas_call(
        functools.partial(last_kernel, factor),
        out_shape=result,
        in_specs=[VMEM] * (1 + spaces) + [HBM],
        out_specs=HBM,
        scratch_shapes=[pltpu.VMEM((own, 2, 2, modes, modes), F32), pltpu.SemaphoreType.DMA((2 * own,))],
        input_output_aliases={1 + spaces: 0},
        compiler_params=PARAMS,
        name="last",
    )(swapped, *late, out)


def turned_rows(mode_rows, momenta, spin_perm, spin_phase, coords, struct_id):
    mode_count = mode_rows.shape[0]
    site_count = mode_rows.shape[2]
    real_part = mode_rows[:, :12, :].astype(F32).reshape(mode_count, 4, 3, site_count)
    imag_part = mode_rows[:, 12:, :].astype(F32).reshape(mode_count, 4, 3, site_count)
    momentum_dot = jnp.sum(momenta[struct_id][:, None] * coords, axis=0)
    quarter = jnp.mod(LAT // 4 * spin_phase[struct_id][:, None] - momentum_dot[None, :], LAT)
    phase_angle = quarter.astype(F32) * (2.0 * math.pi / LAT)
    cosine = jnp.cos(phase_angle)[None, :, None, :]
    sine_val = jnp.sin(phase_angle)[None, :, None, :]
    turn_re = real_part * cosine + imag_part * sine_val
    turn_im = imag_part * cosine - real_part * sine_val
    chooser = (spin_perm[struct_id][:, None] == jnp.arange(4, dtype=jnp.int32)[None, :]).astype(F32)
    moved_re = chooser[0][None, :, None, None] * turn_re[:, 0:1]
    moved_im = chooser[0][None, :, None, None] * turn_im[:, 0:1]
    for a in range(1, 4):
        moved_re = moved_re + chooser[a][None, :, None, None] * turn_re[:, a : a + 1]
        moved_im = moved_im + chooser[a][None, :, None, None] * turn_im[:, a : a + 1]
    re_rows = jnp.concatenate([moved_re, moved_im], axis=1).reshape(mode_count, 24, site_count)
    im_rows = jnp.concatenate([-moved_im, moved_re], axis=1).reshape(mode_count, 24, site_count)
    return jnp.stack([re_rows, im_rows]).astype(BF16).reshape(2 * mode_count, 24 * site_count)


def plain_local(left_modes, right_modes, momenta, spin_perm, spin_phase):
    mode_count, comp_count, site_count = left_modes.shape
    space_count = lax.axis_size("space")
    site_index = lax.axis_index("space") * site_count + lax.iota(jnp.int32, site_count)
    coords = jnp.stack([site_index % BOX, site_index // BOX % BOX, site_index // (BOX * BOX)])
    blocks = [right_modes]
    for _ in range(1, CYCLE):
        blocks.append(routed(blocks[-1], "mode", lambda i: i - 1))
    rights = jnp.stack(blocks).reshape(CYCLE * mode_count, comp_count * site_count)
    all_rows = jnp.concatenate(
        [turned_rows(left_modes, momenta, spin_perm, spin_phase, coords, g) for g in range(STRUCTS)], axis=0
    )
    product = lax.dot_general(all_rows, rights, (((1,), (1,)), ((), ())), preferred_element_type=F32)
    partial_value = product.reshape(STRUCTS, 2, mode_count, CYCLE, mode_count).transpose(0, 3, 1, 2, 4)
    partial_value = partial_value.reshape(STRUCTS * CYCLE * 2, mode_count, mode_count)
    owned = lax.psum_scatter(partial_value, "space", scatter_dimension=0, tiled=True)
    return owned * (1.0 / math.sqrt(24 * site_count * space_count))


def solution(mesh):
    spaces, n_mode = mesh.shape["space"], mesh.shape["mode"]
    fits = spaces & (spaces - 1) == 0 and STRUCTS % spaces == 0 and n_mode % 2 == 0 and n_mode >= CYCLE

    def either(left_modes, *rest):
        body = local if fits and left_modes.shape[2] % LANES == 0 else plain_local
        return body(left_modes, *rest)

    placed = (P("mode", None, "space"), P("mode", None, "space"), P(), P(), P())
    return jax.shard_map(
        either, mesh=mesh, in_specs=placed, out_specs=P("space", "mode", None), check_vma=False
    )
```

```python
import functools
import math

import jax
import jax.numpy as jnp
from jax import lax
from jax.experimental import pallas as pl
from jax.experimental.pallas import tpu as pltpu
from jax.sharding import PartitionSpec as P


STRUCTS = 8
CYCLE = 4
LAT = 96
BOX = 16
LANES = 128
F32 = jnp.float32
BF16 = jnp.bfloat16
VMEM = pl.BlockSpec(memory_space=pltpu.VMEM)
HBM = pl.BlockSpec(memory_space=pltpu.HBM)
PARAMS = pltpu.CompilerParams(vmem_limit_bytes=16 << 20)


def routed(block, axis, source):
    size = lax.axis_size(axis)
    return lax.ppermute(block, axis, [(source(i) % size, i) for i in range(size)])


def turn_tables(momenta, phase, angle, cosine, sine):
    structs = momenta.shape[1]
    sites = angle.shape[1]
    site = lax.axis_index("space") * sites + lax.broadcasted_iota(jnp.int32, (1, sites), 1)
    x = (site % BOX).astype(F32)
    y = (site // BOX % BOX).astype(F32)
    z = (site // (BOX * BOX)).astype(F32)
    for g in range(structs):
        dot = momenta[0, g].astype(F32) * x + momenta[1, g].astype(F32) * y + momenta[2, g].astype(F32) * z
        for a in range(4):
            angle[g * 4 + a : g * 4 + a + 1, :] = (LAT // 4 * phase[a, g]).astype(F32) - dot
    steps = angle[0 : 4 * structs, :]
    steps = steps - LAT * jnp.floor(steps * (1.0 / LAT))
    psi = steps * (2.0 * math.pi / LAT)
    for values, table in ((jnp.cos(psi), cosine), (jnp.sin(psi), sine)):
        angle[0 : 4 * structs, :] = values
        for g in range(0, structs, 2):
            for a in range(4):
                pair = [jnp.broadcast_to(angle[h * 4 + a : h * 4 + a + 1, :], (sites // 2, sites)) for h in (g, g + 1)]
                table[g * 2 + a] = jnp.concatenate(pair, axis=0).T


def turn_rows(left, perm, cosine, sine, rows, turned, piece=32):
    modes = left.shape[0]
    sites = cosine.shape[1]
    half = 12 * sites
    for a in range(4):
        for k in range(3):
            for part in range(2):
                at = part * half + (a * 3 + k) * sites
                value = left[:, at : at + sites].astype(F32)
                turned[part] = jnp.concatenate([value, value], axis=0).T
            for n in range(0, sites, piece):
                re, im = turned[0, n : n + piece], turned[1, n : n + piece]
                for g in range(0, perm.shape[1], 2):
                    co, si = cosine[g * 2 + a, n : n + piece], sine[g * 2 + a, n : n + piece]
                    for base, value in ((0, re * co + im * si), (half, im * co - re * si)):
                        value = value.astype(BF16)
                        for h in range(2):
                            to = pl.multiple_of(base + n + (perm[a, g + h] * 3 + k) * sites, piece)
                            columns = pl.ds((g + h) * modes, modes)
                            rows[pl.ds(to, piece), columns] = value[:, h * modes : (h + 1) * modes]


def flatten(block, flat):
    for at in range(0, block.shape[0], 16):
        flat[at : at + 16, :] = block[at : at + 16].reshape(16, flat.shape[1])


def multiply(all_rows, right, both, total, kept, sends):
    modes, depth = right.shape
    half = depth // 2
    both[0:modes, :] = right[...]
    both[modes:, 0:half] = right[:, half:]
    both[modes:, half:] = -right[:, 0:half]
    me = lax.axis_index("space")
    wide = kept.shape[2]

    def columns(space):
        return pl.ds(pl.multiple_of(space * wide, LANES), wide)

    for slot, rows in enumerate(all_rows):
        total[...] = jnp.dot(both[...], rows[...], preferred_element_type=F32)
        kept[slot] = total[:, columns(me)]
        for distance, send in enumerate(sends, 1):
            send[slot] = total[:, columns(me ^ distance)].astype(BF16)


def first_kernel(n_send, left, right, momenta, perm, phase, rows, cosine, sine, kept, *rest):
    sends, (both, total, angle, lefts, rights, flat, turned, *tables, done) = rest[:n_send], rest[n_send:]
    pairs = list(zip((momenta, perm, phase, left, right), (*tables, lefts, rights)))
    copies = [pltpu.make_async_copy(source, target, done.at[i]) for i, (source, target) in enumerate(pairs)]
    for copy in copies:
        copy.start()
    for copy in copies[:3]:
        copy.wait()
    turn_tables(tables[0], tables[2], angle, cosine, sine)
    copies[3].wait()
    flatten(lefts, flat)
    turn_rows(flat, tables[1], cosine, sine, rows, turned)
    copies[4].wait()
    flatten(rights, flat)
    multiply((rows,), flat, both, total, kept, sends)


def other_kernel(left, perm, cosine, sine, rows, flat, turned, table, done):
    copy = pltpu.make_async_copy(perm, table, done)
    copy.start()
    flatten(left, flat)
    copy.wait()
    turn_rows(flat, table, cosine, sine, rows, turned)


def product_kernel(n_rows, *refs):
    all_rows, (right, kept, *sends, both, total) = refs[:n_rows], refs[n_rows:]
    multiply(all_rows, right, both, total, kept, sends)


def summed(parts, slot):
    value = parts[0][slot]
    for part in parts[1:]:
        value = value + part[slot].astype(F32)
    return value


def planes_of(value, factor, modes):
    turned = (value * factor).T
    halves = range(0, value.shape[0], modes)
    return [[turned[g : g + modes, p : p + modes] for p in halves] for g in range(0, value.shape[1], modes)]


def join_kernel(spaces, factor, *refs):
    early, middle, (out, other) = refs[:spaces], refs[spaces : 2 * spaces], refs[2 * spaces :]
    odd = lax.axis_index("mode") % 2
    other[...] = summed(middle, 1)
    for parts, place in ((early, 0), (middle, 1 + 2 * odd)):
        for g, pair in enumerate(planes_of(summed(parts, 0), factor, out.shape[1])):
            for p in range(2):
                out[(g * CYCLE + place) * 2 + p] = pair[p]


def last_kernel(factor, swapped, *refs):
    late, (_, out, planes, done) = refs[:-4], refs[-4:]
    odd = lax.axis_index("mode") % 2
    copies = []
    for n, place in enumerate((2, 3 - 2 * odd)):
        value = swapped[...] if n == 0 else summed(late, 0)
        for g, pair in enumerate(planes_of(value, factor, out.shape[1])):
            for p in range(2):
                planes[g, n, p] = pair[p]
            to = out.at[pl.ds((g * CYCLE + place) * 2, 2)]
            copies.append(pltpu.make_async_copy(planes.at[g, n], to, done.at[2 * g + n]))
            copies[-1].start()
    for copy in copies:
        copy.wait()


def local(left_modes, right_modes, momenta, spin_perm, spin_phase):
    modes, comps, sites = left_modes.shape
    spaces = lax.axis_size("space")
    depth = comps * sites
    own = STRUCTS // spaces
    n_send = spaces - 1
    shape = jax.ShapeDtypeStruct

    def outs(slots):
        size = (slots, 2 * modes, own * modes)
        return [shape(size, F32)] + [shape(size, BF16)] * n_send

    work = [pltpu.VMEM((2 * modes, depth), BF16), pltpu.VMEM((2 * modes, STRUCTS * modes), F32)]

    ahead = routed(right_modes, "mode", lambda i: i - 1 if i % 2 == 0 else i - 3)
    other_left = routed(left_modes, "mode", lambda i: i ^ 1)
    far = routed(right_modes, "mode", lambda i: i - 3 if i % 2 == 0 else i - 1)
    in_hbm = [pltpu.with_memory_space_constraint(t, pltpu.HBM) for t in (left_modes, right_modes)]
    tables = [pltpu.with_memory_space_constraint(t.T, pltpu.HBM) for t in (momenta, spin_perm, spin_phase)]
    table_shapes = [pltpu.SMEM(t.shape, jnp.int32) for t in tables]
    flat = pltpu.VMEM((modes, depth), BF16)
    turned = pltpu.VMEM((2, sites, 2 * modes), F32)
    rows_shape = shape((depth, STRUCTS * modes), BF16)
    turn_shape = shape((2 * STRUCTS, sites, 2 * modes), F32)

    def exchange(group):
        kept, *sends = group
        return [kept] + [routed(s, "space", lambda i, d=d: i ^ d) for d, s in enumerate(sends, 1)]

    def product(all_rows, block):
        return pl.pallas_call(
            functools.partial(product_kernel, len(all_rows)),
            out_shape=outs(len(all_rows)),
            in_specs=[VMEM] * (len(all_rows) + 1),
            out_specs=[VMEM] * spaces,
            scratch_shapes=work,
            compiler_params=PARAMS,
        )(*all_rows, block.reshape(modes, depth))

    rows, cosine, sine, *group = pl.pallas_call(
        functools.partial(first_kernel, n_send),
        out_shape=[rows_shape, turn_shape, turn_shape] + outs(1),
        in_specs=[HBM] * 5,
        out_specs=[VMEM] * (3 + spaces),
        scratch_shapes=work
        + [pltpu.VMEM((4 * STRUCTS, sites), F32)]
        + [pltpu.VMEM(left_modes.shape, BF16)] * 2
        + [flat, turned]
        + table_shapes
        + [pltpu.SemaphoreType.DMA((5,))],
        compiler_params=PARAMS,
        name="first",
    )(*in_hbm, *tables)
    early = exchange(group)
    other_rows = pl.pallas_call(
        other_kernel,
        out_shape=rows_shape,
        in_specs=[VMEM, HBM, VMEM, VMEM],
        out_specs=VMEM,
        scratch_shapes=[flat, turned, table_shapes[1], pltpu.SemaphoreType.DMA],
        compiler_params=PARAMS,
        name="other",
    )(other_left, tables[1], cosine, sine)
    middle = exchange(product((rows, other_rows), ahead))
    late = exchange(product((rows,), far))
    factor = 1.0 / math.sqrt(depth * spaces)
    result = shape((own * CYCLE * 2, modes, modes), F32)
    out, other = pl.pallas_call(
        functools.partial(join_kernel, spaces, factor),
        out_shape=[result, shape((2 * modes, own * modes), F32)],
        in_specs=[VMEM] * (2 * spaces),
        out_specs=[VMEM] * 2,
        compiler_params=PARAMS,
        name="join",
    )(*early, *middle)
    swapped = routed(other, "mode", lambda i: i ^ 1)
    return pl.pallas_call(
        functools.partial(last_kernel, factor),
        out_shape=result,
        in_specs=[VMEM] * (1 + spaces) + [HBM],
        out_specs=HBM,
        scratch_shapes=[pltpu.VMEM((own, 2, 2, modes, modes), F32), pltpu.SemaphoreType.DMA((2 * own,))],
        input_output_aliases={1 + spaces: 0},
        compiler_params=PARAMS,
        name="last",
    )(swapped, *late, out)


def turned_rows(mode_rows, momenta, spin_perm, spin_phase, coords, struct_id):
    mode_count = mode_rows.shape[0]
    site_count = mode_rows.shape[2]
    real_part = mode_rows[:, :12, :].astype(F32).reshape(mode_count, 4, 3, site_count)
    imag_part = mode_rows[:, 12:, :].astype(F32).reshape(mode_count, 4, 3, site_count)
    momentum_dot = jnp.sum(momenta[struct_id][:, None] * coords, axis=0)
    quarter = jnp.mod(LAT // 4 * spin_phase[struct_id][:, None] - momentum_dot[None, :], LAT)
    phase_angle = quarter.astype(F32) * (2.0 * math.pi / LAT)
    cosine = jnp.cos(phase_angle)[None, :, None, :]
    sine_val = jnp.sin(phase_angle)[None, :, None, :]
    turn_re = real_part * cosine + imag_part * sine_val
    turn_im = imag_part * cosine - real_part * sine_val
    chooser = (spin_perm[struct_id][:, None] == jnp.arange(4, dtype=jnp.int32)[None, :]).astype(F32)
    moved_re = chooser[0][None, :, None, None] * turn_re[:, 0:1]
    moved_im = chooser[0][None, :, None, None] * turn_im[:, 0:1]
    for a in range(1, 4):
        moved_re = moved_re + chooser[a][None, :, None, None] * turn_re[:, a : a + 1]
        moved_im = moved_im + chooser[a][None, :, None, None] * turn_im[:, a : a + 1]
    re_rows = jnp.concatenate([moved_re, moved_im], axis=1).reshape(mode_count, 24, site_count)
    im_rows = jnp.concatenate([-moved_im, moved_re], axis=1).reshape(mode_count, 24, site_count)
    return jnp.stack([re_rows, im_rows]).astype(BF16).reshape(2 * mode_count, 24 * site_count)


def plain_local(left_modes, right_modes, momenta, spin_perm, spin_phase):
    mode_count, comp_count, site_count = left_modes.shape
    space_count = lax.axis_size("space")
    site_index = lax.axis_index("space") * site_count + lax.iota(jnp.int32, site_count)
    coords = jnp.stack([site_index % BOX, site_index // BOX % BOX, site_index // (BOX * BOX)])
    blocks = [right_modes]
    for _ in range(1, CYCLE):
        blocks.append(routed(blocks[-1], "mode", lambda i: i - 1))
    rights = jnp.stack(blocks).reshape(CYCLE * mode_count, comp_count * site_count)
    all_rows = jnp.concatenate(
        [turned_rows(left_modes, momenta, spin_perm, spin_phase, coords, g) for g in range(STRUCTS)], axis=0
    )
    product = lax.dot_general(all_rows, rights, (((1,), (1,)), ((), ())), preferred_element_type=F32)
    partial_value = product.reshape(STRUCTS, 2, mode_count, CYCLE, mode_count).transpose(0, 3, 1, 2, 4)
    partial_value = partial_value.reshape(STRUCTS * CYCLE * 2, mode_count, mode_count)
    owned = lax.psum_scatter(partial_value, "space", scatter_dimension=0, tiled=True)
    return owned * (1.0 / math.sqrt(24 * site_count * space_count))


def solution(mesh):
    spaces, n_mode = mesh.shape["space"], mesh.shape["mode"]
    fits = spaces & (spaces - 1) == 0 and STRUCTS % (2 * spaces) == 0 and n_mode % 2 == 0 and n_mode >= CYCLE

    def either(left_modes, *rest):
        square = left_modes.shape[2] == LANES and 2 * left_modes.shape[0] == LANES
        body = local if fits and square else plain_local
        return body(left_modes, *rest)

    placed = (P("mode", None, "space"), P("mode", None, "space"), P(), P(), P())
    return jax.shard_map(
        either, mesh=mesh, in_specs=placed, out_specs=P("space", "mode", None), check_vma=False
    )
```
